128 devices in a mesh: phase: 4 (over z_hi, core), blk: 32 (over y, z_lo, x).
Axes of the slice: x: 4, y: 4, z: 4 (z_hi: 2, z_lo: 2; z = z_hi * 2 + z_lo), core: 2. Of those that a mesh axis runs over, the one named last changes fastest.
Arguments:
- tokens: bfloat16 [2, 256, 6144], P(None, 'blk'), may hold values from -6 to 6
- norm_gain: float32 [4, 6144], P('phase'), may hold values from 0.5 to 1.5
- up_weight: bfloat16 [4, 6144, 24576], P('phase', None, 'blk'), may hold values from -0.078125 to 0.078125
- up_bias: float32 [4, 24576], P('phase', 'blk'), may hold values from -3 to 3
- down_weight: bfloat16 [4, 24576, 6144], P('phase', 'blk'), may hold values from -0.0390625 to 0.0390625
- down_bias: float32 [4, 6144], P('phase'), may hold values from -3 to 3
Outputs:
- sections: bfloat16 [4, 2, 256, 6144], P('phase', None, 'blk')
The draws below stay inside these ranges and needn't reach their ends.
All inputs are finite; a program needn't handle non-finite values.
Results may differ from the reference program's by a relative error of at most 0.022.
Values may be sent and summed in bfloat16 or wider, within the bound.
A program may use at most 128 MiB of HBM per device.

```python
import jax
import jax.numpy as jnp
from jax import lax

D = 6144
FF = 24576
MICRO = 2
PHASES = 4
TOKENS = 256
N_BLK = 32


def levels(key, dims, split, smallest, largest):
    level = 1.0
    for dim, blocks in split:
        steps = jax.random.uniform(jax.random.fold_in(jax.random.fold_in(key, 6), dim), (blocks,), jnp.float32, smallest / len(split), largest / len(split))
        level = level * jnp.repeat(jnp.exp(steps), dims[dim] // blocks).reshape((-1,) + (1,) * (len(dims) - 1 - dim))
    return level


def gaussian(own_key, shape, width, reach, split=(), kind=jnp.bfloat16):
    factor_of = levels(own_key, shape, split, -0.22, 0.18) if split else 1.0
    values = jax.random.normal(own_key, shape, jnp.float32) * width * factor_of
    return jnp.minimum(jnp.maximum(values, -reach), reach).astype(kind)


def setup_inputs(seed: int = 0) -> dict:
    keys = jax.random.split(jax.random.key(seed), 7)
    tokens = gaussian(keys[0], (MICRO, TOKENS, D), 1.0, 6.0, ((1, 32),))
    norm_gain = jnp.clip(0.5 + 1.0 * jax.random.uniform(keys[1], (PHASES, D), jnp.float32) ** levels(keys[1], (PHASES, D), ((0, 4),), -0.2, 0.2), 0.5, 1.5)
    up_weight = gaussian(keys[2], (PHASES, D, FF), D ** -0.5, 0.078125, ((0, 4), (2, 32)))
    up_bias = gaussian(keys[3], (PHASES, FF), 0.5, 3.0, ((0, 4), (1, 32)), jnp.float32)
    down_weight = gaussian(keys[4], (PHASES, FF, D), FF ** -0.5, 0.0390625, ((0, 4), (1, 32)))
    down_bias = gaussian(keys[5], (PHASES, D), 0.5, 3.0, ((0, 4),), jnp.float32)
    return {"tokens": tokens, "norm_gain": norm_gain, "up_weight": up_weight, "up_bias": up_bias, "down_weight": down_weight, "down_bias": down_bias}


def section_layer(inputs, gain_row, w_up, b_up, w_down, b_down):
    widened = inputs.astype(jnp.float32)
    row_mean = lax.optimization_barrier(jnp.mean(widened, axis=-1, keepdims=True))
    centered = widened - row_mean
    row_var = lax.optimization_barrier(jnp.mean(centered * centered, axis=-1, keepdims=True))
    normed = (centered * lax.rsqrt(row_var + 1e-05) * gain_row).astype(jnp.bfloat16)
    hidden = jax.nn.gelu(jnp.dot(normed, w_up, preferred_element_type=jnp.float32) + b_up).astype(jnp.bfloat16)
    row_count = hidden.shape[0]
    blocks_hidden = jnp.moveaxis(hidden.reshape(row_count, N_BLK, FF // N_BLK), 1, 0)
    blocks_weight = w_down.reshape(N_BLK, FF // N_BLK, D)

    def accumulate(total, pair):
        part = jnp.dot(pair[0], pair[1], preferred_element_type=jnp.float32).astype(jnp.bfloat16)
        part = lax.optimization_barrier(part)
        return (total + part.astype(jnp.float32), None)
    start_total = jnp.zeros((row_count, D), jnp.float32)
    branch, unused = lax.scan(accumulate, start_total, (blocks_hidden, blocks_weight))
    return (widened + branch + b_down).astype(jnp.bfloat16)

def reference(tokens, norm_gain, up_weight, up_bias, down_weight, down_bias):
    collected = []
    current = [tokens[index] for index in range(MICRO)]
    for level in range(PHASES):
        current = [section_layer(current[index], norm_gain[level], up_weight[level], up_bias[level], down_weight[level], down_bias[level]) for index in range(MICRO)]
        collected.append(jnp.stack(current))
    return jnp.stack(collected)
```

```python
import functools

import jax
import jax.numpy as jnp
from jax import lax
from jax.experimental import pallas as pl
from jax.experimental.pallas import tpu as pltpu
from jax.sharding import PartitionSpec as P

MESH = pl.DeviceIdType.MESH
SIDE = 4
F32, BF16 = jnp.float32, jnp.bfloat16


def kernel(phases, tokens, gain, b_up, b_down, w_up_hbm, w_down_hbm, out,
           w_up, w_down, x_in, gathered, hidden, partial, far1, near1, sum1, far2, near2,
           z_own, z_got, x_out,
           w_sem, zx_sem, in_sem, ag_send, ag_recv, rs_send, rs_recv, z_send, z_recv, next_send):
    micro, _, depth = tokens.shape
    quarter = depth // 4
    half = depth // 2
    units = w_up.shape[1]
    rows = 16 * SIDE * SIDE
    phase = lax.axis_index("phase")
    blk = lax.axis_index("blk")
    y, z, x = blk // 8, (blk // 4) % 2, blk % 4

    def at(yy, zz, xx):
        return (phase, ((yy % SIDE) * 2 + zz) * 4 + xx % SIDE)

    def turned(where, odd):
        return jnp.where(odd == 1, y * 8 + (1 - z) * 4 + x, where)

    step_to = {("x", 1): at(y, z, x + 1), ("x", -1): at(y, z, x + 3),
               ("y", 1): at(y + 1, z, x), ("y", -1): at(y + 3, z, x)}
    z_peer = at(y, 1 - z, x)
    after = ((phase + 1) % phases, turned(blk, phase % 2))
    before = ((phase + phases - 1) % phases, turned(blk, (phase + 1) % 2))

    up_copy = pltpu.make_async_copy(w_up_hbm.at[0], w_up, w_sem.at[0])
    down_copy = pltpu.make_async_copy(w_down_hbm.at[0], w_down, w_sem.at[1])
    up_copy.start()
    down_copy.start()

    barrier = pltpu.get_barrier_semaphore()
    friends = list(step_to.values()) + [z_peer, after, before]
    for friend in friends:
        pl.semaphore_signal(barrier, inc=1, device_id=friend, device_id_type=MESH)
    pl.semaphore_wait(barrier, len(friends))

    def zx_copy(m):
        return pltpu.make_async_remote_copy(
            src_ref=tokens.at[m], dst_ref=x_in.at[m, z], send_sem=zx_sem.at[m], recv_sem=in_sem.at[m],
            device_id=z_peer, device_id_type=MESH)

    def next_copy(m):
        return pltpu.make_async_remote_copy(
            src_ref=x_out.at[m], dst_ref=x_in.at[m], send_sem=next_send.at[m], recv_sem=in_sem.at[m],
            device_id=after, device_id_type=MESH)

    @pl.when(phase == 0)
    def _():
        for m in range(micro):
            zx_copy(m).start()
        for m in range(micro):
            x_in[m, z] = tokens[m]

    def send(src, dst, send_sem, recv_sem, device):
        copy = pltpu.make_async_remote_copy(src_ref=src, dst_ref=dst, send_sem=send_sem, recv_sem=recv_sem,
                                            device_id=device, device_id_type=MESH)
        copy.start()
        return copy

    def one(m, carry):
        @pl.when(phase == 0)
        def _():
            zx_copy(m).wait_recv()

        @pl.when(phase > 0)
        def _():
            next_copy(m).wait_recv()

        normed = []
        for row in range(2):
            wide = x_in[m, row].astype(F32)
            mean = jnp.mean(wide, axis=-1, keepdims=True)
            centered = wide - mean
            var = jnp.mean(centered * centered, axis=-1, keepdims=True)
            normed.append(centered * lax.rsqrt(var + 1e-05) * gain[...])
        gathered[m, y, x] = jnp.concatenate(normed, axis=0).astype(BF16)

        sends = []
        first_axis, second_axis = ("x", "y"), ("y", "x")
        first, second = (x, y), (y, x)

        def slot(h, s, f):
            return gathered.at[m, s % SIDE, f % SIDE] if h == 0 else gathered.at[m, f % SIDE, s % SIDE]

        def spread(h, s, f, start, size, axis, way, index):
            block = slot(h, s, f).at[:, pl.ds(start, size)]
            d = 0 if way == 1 else 1
            sends.append(send(block, block, ag_send.at[h, d, index], ag_recv.at[m, h, d, index], step_to[axis, way]))

        def arrived(h, d, index, size):
            block = gathered.at[m, 0, 0, :, pl.ds(0, size)]
            pltpu.make_async_remote_copy(src_ref=block, dst_ref=block, send_sem=ag_send.at[h, d, index],
                                         recv_sem=ag_recv.at[m, h, d, index], device_id=z_peer,
                                         device_id_type=MESH).wait_recv()

        for h in range(2):
            for way in (1, -1):
                spread(h, second[h], first[h], h * half, half, first_axis[h], way, 0)
        for h in range(2):
            for way in (1, -1):
                spread(h, second[h], first[h], h * half, half, second_axis[h], way, 2)
        for d, way in ((0, 1), (1, -1)):
            for h in range(2):
                arrived(h, d, 0, half)
                spread(h, second[h], first[h] + (SIDE - way), h * half + d * quarter, quarter, first_axis[h], way, 1)
        for d, way in ((0, 1), (1, -1)):
            for h in range(2):
                for to in (1, -1):
                    spread(h, second[h], first[h] + (SIDE - way), h * half, half, second_axis[h], to, 3 + d)
        for h in range(2):
            arrived(h, 0, 1, quarter)
            arrived(h, 1, 1, quarter)
            for to in (1, -1):
                spread(h, second[h], first[h] + 2, h * half, half, second_axis[h], to, 5)
        shift = (0, SIDE - 1, 1, 2)
        for index in range(4):
            for d, way in ((0, 1), (1, -1)):
                for h in range(2):
                    arrived(h, d, 2 + index, half)
                    spread(h, second[h] + (SIDE - way), first[h] + shift[index], h * half + d * quarter, quarter,
                           second_axis[h], way, 6 + index)
        for index in range(4):
            for d in range(2):
                for h in range(2):
                    arrived(h, d, 6 + index, quarter)

        @pl.when(m == 0)
        def _():
            up_copy.wait()

        wide_n = min(256, units)

        def up(n, c):
            columns = pl.ds(pl.multiple_of(n * wide_n, wide_n), wide_n)
            block = gathered[m].reshape(rows, depth)
            value = jnp.dot(block, w_up[:, columns], preferred_element_type=F32) + b_up[:, columns]
            hidden[:, columns] = jax.nn.gelu(value).astype(BF16)
            return c

        lax.fori_loop(0, units // wide_n, up, 0)

        @pl.when(m == 0)
        def _():
            down_copy.wait()

        wide_q = min(512, quarter)

        def strip(h, s, start, size):
            cut = pl.ds(start, size)
            return partial.at[m, s % SIDE, :, :, cut] if h == 0 else partial.at[m, :, s % SIDE, :, cut]

        def reduce1(h, src, dst, way, index):
            d = 0 if way == 1 else 1
            sends.append(send(src, dst, rs_send.at[h, 0, d, index], rs_recv.at[m, h, 0, d, index],
                              step_to[second_axis[h], way]))

        def reduce2(h, src, dst, way, index):
            d = 0 if way == 1 else 1
            sends.append(send(src, dst, rs_send.at[h, 1, d, index], rs_recv.at[m, h, 1, d, index],
                              step_to[first_axis[h], way]))

        def got(ref, h, stage, d, index):
            pltpu.make_async_remote_copy(src_ref=ref, dst_ref=ref, send_sem=rs_send.at[h, stage, d, index],
                                         recv_sem=rs_recv.at[m, h, stage, d, index], device_id=z_peer,
                                         device_id_type=MESH).wait_recv()

        for d, way in ((0, 1), (1, -1)):
            for h in range(2):
                base = h * half + d * quarter

                def down(n, c):
                    columns = pl.ds(pl.multiple_of(base + n * wide_q, wide_q), wide_q)
                    value = jnp.dot(hidden[...], w_down[:, columns], preferred_element_type=F32)
                    partial[m, :, :, :, columns] = value.astype(BF16).reshape(SIDE, SIDE, 16, wide_q)
                    return c

                lax.fori_loop(0, quarter // wide_q, down, 0)
                reduce1(h, strip(h, second[h] + 2, base, quarter), far1.at[m, h, d], way, 0)
                reduce1(h, strip(h, second[h] + way + SIDE * 0 + (SIDE - 2 * way), base, quarter),
                        near1.at[m, h, 1 - d, d], -way, 1 + d)
        for d, way in ((0, 1), (1, -1)):
            for h in range(2):
                base = h * half + d * quarter
                got(far1.at[m, h, d], h, 0, d, 0)
                target = strip(h, second[h] + SIDE + way, base, quarter)

                def fold(i, c):
                    target[i] = (target[i].astype(F32) + far1[m, h, d, i].astype(F32)).astype(BF16)
                    return c

                lax.fori_loop(0, SIDE, fold, 0)
                reduce1(h, target, near1.at[m, h, d, d], way, 1 + d)
        for h in range(2):
            for part in range(2):
                for d in range(2):
                    got(near1.at[m, h, d, part], h, 0, d, 1 + part)
                mine = strip(h, second[h], h * half + part * quarter, quarter)

                def fold(i, c):
                    total = mine[i].astype(F32) + near1[m, h, 0, part, i].astype(F32) + near1[m, h, 1, part, i].astype(F32)
                    sum1[m, h, part, i] = total.astype(BF16)
                    return c

                lax.fori_loop(0, SIDE, fold, 0)
                way = 1 - 2 * part
                f = first[h]
                reduce2(h, sum1.at[m, h, part, (f + 2) % SIDE], far2.at[m, h, part], way, 0)
                reduce2(h, sum1.at[m, h, part, (f + SIDE - way) % SIDE], near2.at[m, h, 1 - part, part], -way, 1 + part)
        for h in range(2):
            for d, way in ((0, 1), (1, -1)):
                got(far2.at[m, h, d], h, 1, d, 0)
                target = sum1.at[m, h, d, (first[h] + SIDE + way) % SIDE]
                target[...] = (target[...].astype(F32) + far2[m, h, d].astype(F32)).astype(BF16)
                reduce2(h, target, near2.at[m, h, d, d], way, 1 + d)
        z_copies = []
        for h in range(2):
            for part in range(2):
                for d in range(2):
                    got(near2.at[m, h, d, part], h, 1, d, 1 + part)
                total = (sum1[m, h, part, first[h]].astype(F32) + near2[m, h, 0, part].astype(F32)
                         + near2[m, h, 1, part].astype(F32))
                z_own[m, 2 * h + part] = total.astype(BF16)
                z_copies.append(send(z_own.at[m, 2 * h + part], z_got.at[m, 2 * h + part], z_send.at[2 * h + part],
                                     z_recv.at[m, 2 * h + part], z_peer))
        for q in range(4):
            z_copies[q].wait_recv()
            branch = z_own[m, q].astype(F32) + z_got[m, q].astype(F32)
            columns = pl.ds(q * quarter, quarter)
            for row in range(2):
                value = x_in[m, row, :, columns].astype(F32) + branch[8 * row:8 * row + 8] + b_down[:, columns]
                x_out[m, row, :, columns] = value.astype(BF16)

        @pl.when(phase < phases - 1)
        def _():
            next_copy(m).start()

        out[0, m] = x_out[m, z]
        for copy in sends + z_copies:
            copy.wait_send()
        return carry

    lax.fori_loop(0, micro, one, 0)

    @pl.when(phase == 0)
    def _():
        for m in range(micro):
            zx_copy(m).wait_send()

    @pl.when(phase < phases - 1)
    def _():
        for m in range(micro):
            next_copy(m).wait_send()


def on_device(phases, tokens, norm_gain, up_weight, up_bias, down_weight, down_bias):
    micro, own, depth = tokens.shape
    units = up_weight.shape[2]
    quarter = depth // 4
    vmem = pl.BlockSpec(memory_space=pltpu.VMEM)
    hbm = pl.BlockSpec(memory_space=pl.ANY)
    dma = pltpu.SemaphoreType.DMA
    return pl.pallas_call(
        functools.partial(kernel, phases),
        out_shape=jax.ShapeDtypeStruct((1, micro, own, depth), BF16),
        in_specs=[vmem, vmem, vmem, vmem, hbm, hbm],
        out_specs=vmem,
        scratch_shapes=[
            pltpu.VMEM((depth, units), BF16),
            pltpu.VMEM((units, depth), BF16),
            pltpu.VMEM((micro, 2, own, depth), BF16),
            pltpu.VMEM((micro, SIDE, SIDE, 16, depth), BF16),
            pltpu.VMEM((16 * SIDE * SIDE, units), BF16),
            pltpu.VMEM((micro, SIDE, SIDE, 16, depth), BF16),
            pltpu.VMEM((micro, 2, 2, SIDE, 16, quarter), BF16),
            pltpu.VMEM((micro, 2, 2, 2, SIDE, 16, quarter), BF16),
            pltpu.VMEM((micro, 2, 2, SIDE, 16, quarter), BF16),
            pltpu.VMEM((micro, 2, 2, 16, quarter), BF16),
            pltpu.VMEM((micro, 2, 2, 2, 16, quarter), BF16),
            pltpu.VMEM((micro, 4, 16, quarter), BF16),
            pltpu.VMEM((micro, 4, 16, quarter), BF16),
            pltpu.VMEM((micro, 2, own, depth), BF16),
            dma((2,)),
            dma((micro,)),
            dma((micro,)),
            dma((2, 2, 10)),
            dma((micro, 2, 2, 10)),
            dma((2, 2, 2, 3)),
            dma((micro, 2, 2, 2, 3)),
            dma((4,)),
            dma((micro, 4)),
            dma((micro,)),
        ],
        compiler_params=pltpu.CompilerParams(
            collective_id=0, has_side_effects=True, vmem_limit_bytes=60 * 1024 * 1024),
        name="relay",
    )(tokens, norm_gain, up_bias, down_bias, up_weight, down_weight)


def solution(mesh):
    return jax.shard_map(
        functools.partial(on_device, mesh.shape["phase"]),
        mesh=mesh,
        in_specs=(
            P(None, "blk", None),
            P("phase", None),
            P("phase", None, "blk"),
            P("phase", "blk"),
            P("phase", "blk", None),
            P("phase", None),
        ),
        out_specs=P("phase", None, "blk", None),
        check_vma=False,
    )
```

```python
import functools

import jax
import jax.numpy as jnp
from jax import lax
from jax.experimental import pallas as pl
from jax.experimental.pallas import tpu as pltpu
from jax.sharding import PartitionSpec as P

MESH = pl.DeviceIdType.MESH
SIDE = 4
ROWS = 8
F32, BF16 = jnp.float32, jnp.bfloat16
ORDER = (
    "X0", "X1", "a0", "b0", "c0", "e0", "a1", "b1", "c1", "f0", "e1", "g0", "h0", "X2", "X3", "G0",
    "f1", "g1", "a2", "h1", "b2", "c2", "U0", "a3", "e2", "D0", "E0", "f2", "G1", "b3", "g2", "U1",
    "h2", "c3", "D1", "m0", "E1", "n0", "G2", "e3", "f3", "g3", "h3", "U2", "m1", "n1", "D2", "p0",
    "r0", "E2", "G3", "U3", "p1", "r1", "D3", "m2", "E3", "q0", "s0", "n2", "m3", "q1", "s1", "n3",
    "Z0", "p2", "r2", "Z1", "p3", "r3", "q2", "s2", "q3", "s3", "Z2", "Z3",
)


def kernel(phases, tokens, gain, b_up, b_down, w_up_hbm, w_down_hbm, out,
           w_up, w_down, x_in, gathered, lhs, hidden, partial, far1, near1, sum1, near2, z_own, z_got, x_out,
           w_sem, zx_sem, in_sem, ag1_send, ag1_recv, ag2_send, ag2_recv, ag3_send, ag3_recv, rs_send, rs_recv, z_send, z_recv, next_send):
    micro, _, depth = tokens.shape
    chunks = 2 * micro
    quarter = depth // 4
    half = depth // 2
    units = w_up.shape[1]
    rows = ROWS * SIDE * SIDE
    phase = lax.axis_index("phase")
    blk = lax.axis_index("blk")
    y, z, x = blk // 8, (blk // 4) % 2, blk % 4

    def at(yy, zz, xx):
        return (phase, ((yy % SIDE) * 2 + zz) * 4 + xx % SIDE)

    def turned(odd):
        return jnp.where(odd == 1, y * 8 + (1 - z) * 4 + x, blk)

    def along(axis, t):
        return at(y, z, x + t) if axis == "x" else at(y + t, z, x)

    z_peer = at(y, 1 - z, x)
    after = ((phase + 1) % phases, turned(phase % 2))
    before = ((phase + phases - 1) % phases, turned((phase + 1) % 2))

    up_copy = pltpu.make_async_copy(w_up_hbm.at[0], w_up, w_sem.at[0])
    down_copy = pltpu.make_async_copy(w_down_hbm.at[0], w_down, w_sem.at[1])
    up_copy.start()
    down_copy.start()

    barrier = pltpu.get_barrier_semaphore()
    friends = [along(axis, t) for axis in "xy" for t in (1, 2, 3)] + [z_peer, after, before]
    for friend in friends:
        pl.semaphore_signal(barrier, inc=1, device_id=friend, device_id_type=MESH)
    pl.semaphore_wait(barrier, len(friends))

    def remote(src, dst, send_sem, recv_sem, device):
        return pltpu.make_async_remote_copy(src_ref=src, dst_ref=dst, send_sem=send_sem, recv_sem=recv_sem,
                                            device_id=device, device_id_type=MESH)

    def zx_copy(m):
        c = 2 * m + z
        return remote(tokens.at[m], x_in.at[c], zx_sem.at[m], in_sem.at[c], z_peer)

    def next_copy(c):
        return remote(x_out.at[c], x_in.at[c], next_send.at[c], in_sem.at[c], after)

    @pl.when(phase == 0)
    def _():
        for m in range(micro):
            zx_copy(m).start()
        for m in range(micro):
            x_in[2 * m + z] = tokens[m]

    sends = []

    def send(*args):
        copy = remote(*args)
        copy.start()
        sends.append(copy)

    first_axis, second_axis = ("x", "y"), ("y", "x")
    first, second = (x, y), (y, x)
    HOPS = (2, 1, 3)
    WAY = (1, 3)

    def slot(c, h, s, f):
        return gathered.at[c, s % SIDE, f % SIDE] if h == 0 else gathered.at[c, f % SIDE, s % SIDE]

    def enter(c):
        @pl.when((phase == 0) & (z != c % 2))
        def _():
            remote(tokens.at[c // 2], x_in.at[c], zx_sem.at[c // 2], in_sem.at[c], z_peer).wait_recv()

        @pl.when(phase > 0)
        def _():
            next_copy(c).wait_recv()

        wide = x_in[c].astype(F32)
        mean = jnp.mean(wide, axis=-1, keepdims=True)
        centered = wide - mean
        var = jnp.mean(centered * centered, axis=-1, keepdims=True)
        gathered[c, y, x] = (centered * lax.rsqrt(var + 1e-05) * gain[...]).astype(BF16)
        for t in HOPS:
            for h in range(2):
                block = slot(c, h, second[h], first[h]).at[:, pl.ds(h * half, half)]
                send(block, block, ag1_send.at[c, h, t - 1], ag1_recv.at[c, h, t - 1], along(first_axis[h], t))
        for h in range(2):
            relay(c, h, 0)

    def near_block(c, h, back):
        return slot(c, h, second[h], first[h] + SIDE - back).at[:, pl.ds(h * half, half)]

    def relay(c, h, back):
        block = near_block(c, h, back)
        for d in range(2):
            send(block, block, ag2_send.at[c, h, d, back], ag2_recv.at[c, h, d, back], along(second_axis[h], WAY[d]))

    def pass_on(c, back):
        for h in range(2):
            block = slot(c, h, 0, 0).at[:, pl.ds(0, half)]
            remote(block, block, ag1_send.at[c, h, back - 1], ag1_recv.at[c, h, back - 1], z_peer).wait_recv()
            relay(c, h, back)

    def forward(c, back):
        for d in range(2):
            for h in range(2):
                block = slot(c, h, 0, 0).at[:, pl.ds(0, half)]
                remote(block, block, ag2_send.at[c, h, d, back], ag2_recv.at[c, h, d, back], z_peer).wait_recv()
                block = slot(c, h, second[h] + SIDE - WAY[d], first[h] + SIDE - back).at[:, pl.ds(h * half + d * quarter, quarter)]
                send(block, block, ag3_send.at[c, h, d, back], ag3_recv.at[c, h, d, back], along(second_axis[h], WAY[d]))

    def collect(c):
        for back in range(SIDE):
            for d in range(2):
                for h in range(2):
                    block = slot(c, h, 0, 0).at[:, pl.ds(0, quarter)]
                    remote(block, block, ag3_send.at[c, h, d, back], ag3_recv.at[c, h, d, back], z_peer).wait_recv()

        def pack(i, carry):
            yy, xx = i // 2, (i % 2) * 2
            pair = jnp.concatenate([gathered[c, yy, xx].astype(F32), gathered[c, yy, xx + 1].astype(F32)], axis=0)
            lhs[pl.ds(pl.multiple_of(i * 2 * ROWS, 2 * ROWS), 2 * ROWS), :] = pair.astype(BF16)
            return carry

        lax.fori_loop(0, rows // (2 * ROWS), pack, 0)

    def up(c):
        if c == 0:
            up_copy.wait()
        wide_n = min(256, units)

        def tile(n, carry):
            columns = pl.ds(pl.multiple_of(n * wide_n, wide_n), wide_n)
            value = jnp.dot(lhs[...], w_up[:, columns], preferred_element_type=F32) + b_up[:, columns]
            hidden[:, columns] = jax.nn.gelu(value).astype(BF16)
            return carry

        lax.fori_loop(0, units // wide_n, tile, 0)

    def strip(c, h, part, s):
        return partial.at[c, h, part, s % SIDE]

    def reduce_send(c, h, stage, src, dst, d, index):
        send(src, dst, rs_send.at[c, h, stage, d, index], rs_recv.at[c, h, stage, d, index],
             along(second_axis[h], WAY[d]))

    def got(c, h, stage, d, index, ref):
        remote(ref, ref, rs_send.at[c, h, stage, d, index], rs_recv.at[c, h, stage, d, index], z_peer).wait_recv()

    def down(c, part):
        if c == 0 and part == 0:
            down_copy.wait()
        wide_q = min(512, quarter)
        for h in range(2):
            base = h * half + part * quarter

            def tile(n, carry):
                start = pl.multiple_of(n * wide_q, wide_q)
                value = jnp.dot(hidden[...], w_down[:, pl.ds(base + start, wide_q)], preferred_element_type=F32)
                value = value.reshape(SIDE, SIDE, ROWS, wide_q).astype(BF16)
                for i in range(SIDE):
                    if h == 0:
                        partial[c, h, part, i, :, :, pl.ds(start, wide_q)] = value[i]
                    else:
                        partial[c, h, part, :, i, :, pl.ds(start, wide_q)] = value[i]
                return carry

            lax.fori_loop(0, quarter // wide_q, tile, 0)
            reduce_send(c, h, 0, strip(c, h, part, second[h] + 2), far1.at[c, h, part], part, 0)
            reduce_send(c, h, 0, strip(c, h, part, second[h] + WAY[1 - part]), near1.at[c, h, 1 - part, part],
                        1 - part, 1 + part)

    def merge(c, part):
        for h in range(2):
            got(c, h, 0, part, 0, far1.at[c, h, part])
            target = strip(c, h, part, second[h] + WAY[part])

            def fold(i, carry):
                target[i] = (target[i].astype(F32) + far1[c, h, part, i].astype(F32)).astype(BF16)
                return carry

            lax.fori_loop(0, SIDE, fold, 0)
            reduce_send(c, h, 0, target, near1.at[c, h, part, part], part, 1 + part)

    def reduce1(c, part):
        for h in range(2):
            for d in range(2):
                got(c, h, 0, d, 1 + part, near1.at[c, h, d, part])
            mine = strip(c, h, part, second[h])

            def fold(i, carry):
                total = mine[i].astype(F32)
                for d in range(2):
                    total = total + near1[c, h, d, part, i].astype(F32)
                sum1[c, h, part, i] = total.astype(BF16)
                return carry

            lax.fori_loop(0, SIDE, fold, 0)
            for t in HOPS:
                send(sum1.at[c, h, part, (first[h] + t) % SIDE], near2.at[c, h, t - 1, part],
                     rs_send.at[c, h, 1, t - 1, part], rs_recv.at[c, h, 1, t - 1, part], along(first_axis[h], t))

    def z_copy(c, h, part):
        return remote(z_own.at[c, h, part], z_got.at[c, h, part], z_send.at[c, h, part], z_recv.at[c, h, part], z_peer)

    def reduce2(c, part):
        if True:
            for h in range(2):
                for t in HOPS:
                    ref = near2.at[c, h, t - 1, part]
                    remote(ref, ref, rs_send.at[c, h, 1, t - 1, part], rs_recv.at[c, h, 1, t - 1, part], z_peer).wait_recv()
                total = sum1[c, h, part, first[h]].astype(F32)
                for t in range(3):
                    total = total + near2[c, h, t, part].astype(F32)
                z_own[c, h, part] = total.astype(BF16)
                copy = z_copy(c, h, part)
                copy.start()
                sends.append(copy)

    def leave(c):
        for part in range(2):
            for h in range(2):
                z_copy(c, h, part).wait_recv()
                branch = z_own[c, h, part].astype(F32) + z_got[c, h, part].astype(F32)
                columns = pl.ds(h * half + part * quarter, quarter)
                x_out[c, :, columns] = (x_in[c, :, columns].astype(F32) + branch + b_down[:, columns]).astype(BF16)

        @pl.when(phase < phases - 1)
        def _():
            next_copy(c).start()

        @pl.when(z == c % 2)
        def _():
            out[0, c // 2] = x_out[c]

    steps = {"X": (enter,), "a": (pass_on, 1), "b": (pass_on, 3), "c": (pass_on, 2), "G": (collect,), "U": (up,), "D": (down, 0), "E": (down, 1),
             "e": (forward, 0), "f": (forward, 1), "g": (forward, 3), "h": (forward, 2), "m": (merge, 0), "n": (merge, 1),
             "p": (reduce1, 0), "r": (reduce1, 1), "q": (reduce2, 0), "s": (reduce2, 1), "Z": (leave,)}
    for step in ORDER:
        fn, *more = steps[step[0]]
        fn(int(step[1]), *more)

    for copy in sends:
        copy.wait_send()

    @pl.when(phase == 0)
    def _():
        for m in range(micro):
            zx_copy(m).wait_send()

    @pl.when(phase < phases - 1)
    def _():
        for c in range(chunks):
            next_copy(c).wait_send()


def on_device(phases, tokens, norm_gain, up_weight, up_bias, down_weight, down_bias):
    micro, own, depth = tokens.shape
    units = up_weight.shape[2]
    quarter = depth // 4
    chunks = 2 * micro
    vmem = pl.BlockSpec(memory_space=pltpu.VMEM)
    hbm = pl.BlockSpec(memory_space=pl.ANY)
    dma = pltpu.SemaphoreType.DMA
    return pl.pallas_call(
        functools.partial(kernel, phases),
        out_shape=jax.ShapeDtypeStruct((1, micro, own, depth), BF16),
        in_specs=[vmem, vmem, vmem, vmem, hbm, hbm],
        out_specs=vmem,
        scratch_shapes=[
            pltpu.VMEM((depth, units), BF16),
            pltpu.VMEM((units, depth), BF16),
            pltpu.VMEM((chunks, ROWS, depth), BF16),
            pltpu.VMEM((chunks, SIDE, SIDE, ROWS, depth), BF16),
            pltpu.VMEM((ROWS * SIDE * SIDE, depth), BF16),
            pltpu.VMEM((ROWS * SIDE * SIDE, units), BF16),
            pltpu.VMEM((chunks, 2, 2, SIDE, SIDE, ROWS, quarter), BF16),
            pltpu.VMEM((chunks, 2, 2, SIDE, ROWS, quarter), BF16),
            pltpu.VMEM((chunks, 2, 2, 2, SIDE, ROWS, quarter), BF16),
            pltpu.VMEM((chunks, 2, 2, SIDE, ROWS, quarter), BF16),
            pltpu.VMEM((chunks, 2, 3, 2, ROWS, quarter), BF16),
            pltpu.VMEM((chunks, 2, 2, ROWS, quarter), BF16),
            pltpu.VMEM((chunks, 2, 2, ROWS, quarter), BF16),
            pltpu.VMEM((chunks, ROWS, depth), BF16),
            dma((2,)),
            dma((micro,)),
            dma((chunks,)),
            dma((chunks, 2, 3)),
            dma((chunks, 2, 3)),
            dma((chunks, 2, 2, 4)),
            dma((chunks, 2, 2, 4)),
            dma((chunks, 2, 2, 4)),
            dma((chunks, 2, 2, 4)),
            dma((chunks, 2, 2, 3, 3)),
            dma((chunks, 2, 2, 3, 3)),
            dma((chunks, 2, 2)),
            dma((chunks, 2, 2)),
            dma((chunks,)),
        ],
        compiler_params=pltpu.CompilerParams(
            collective_id=0, has_side_effects=True, vmem_limit_bytes=60 * 1024 * 1024),
        name="relay",
    )(tokens, norm_gain, up_bias, down_bias, up_weight, down_weight)


def solution(mesh):
    return jax.shard_map(
        functools.partial(on_device, mesh.shape["phase"]),
        mesh=mesh,
        in_specs=(
            P(None, "blk", None),
            P("phase", None),
            P("phase", None, "blk"),
            P("phase", "blk"),
            P("phase", "blk", None),
            P("phase", None),
        ),
        out_specs=P("phase", None, "blk", None),
        check_vma=False,
    )
```

```python
import functools

import jax
import jax.numpy as jnp
from jax import lax
from jax.experimental import pallas as pl
from jax.experimental.pallas import tpu as pltpu
from jax.sharding import PartitionSpec as P

MESH = pl.DeviceIdType.MESH
SIDE = 4
ROWS = 8
F32, BF16 = jnp.float32, jnp.bfloat16
ORDER = (
    "X0", "X1", "a0", "b0", "c0", "e0", "a1", "X2", "f0", "g0", "h0", "b1", "c1", "e1", "a2", "b2",
    "c2", "X3", "G0", "f1", "U0", "g1", "h1", "e2", "D0", "a3", "b3", "c3", "f2", "g2", "h2", "E0",
    "G1", "U1", "e3", "D1", "f3", "m0", "g3", "h3", "E1", "G2", "U2", "n0", "m1", "D2", "E2", "G3",
    "n1", "U3", "p1", "p0", "r0", "D3", "m2", "r1", "n2", "E3", "q0", "s0", "q1", "m3", "p2", "s1",
    "r2", "Z0", "n3", "Z1", "q2", "p3", "s2", "r3", "Z2", "q3", "s3", "Z3",
)


def kernel(phases, tokens, gain, b_up, b_down, w_up_hbm, w_down_hbm, out,
           w_up, w_down, x_in, gathered, lhs, hidden, partial, far1, near1, sum1, near2, z_own, z_got, x_out,
           w_sem, zx_sem, in_sem, ag1_send, ag1_recv, ag2_send, ag2_recv, ag3_send, ag3_recv, rs_send, rs_recv, z_send, z_recv, next_send):
    micro, _, depth = tokens.shape
    chunks = 2 * micro
    quarter = depth // 4
    half = depth // 2
    units = w_up.shape[1]
    rows = ROWS * SIDE * SIDE
    phase = lax.axis_index("phase")
    blk = lax.axis_index("blk")
    y, z, x = blk // 8, (blk // 4) % 2, blk % 4

    def at(yy, zz, xx):
        return (phase, ((yy % SIDE) * 2 + zz) * 4 + xx % SIDE)

    def turned(odd):
        return jnp.where(odd == 1, y * 8 + (1 - z) * 4 + x, blk)

    def along(axis, t):
        return at(y, z, x + t) if axis == "x" else at(y + t, z, x)

    z_peer = at(y, 1 - z, x)
    after = ((phase + 1) % phases, turned(phase % 2))
    before = ((phase + phases - 1) % phases, turned((phase + 1) % 2))

    up_copy = pltpu.make_async_copy(w_up_hbm.at[0], w_up, w_sem.at[0])
    down_copy = pltpu.make_async_copy(w_down_hbm.at[0], w_down, w_sem.at[1])
    up_copy.start()
    down_copy.start()

    barrier = pltpu.get_barrier_semaphore()
    friends = [along(axis, t) for axis in "xy" for t in (1, 2, 3)] + [z_peer, after, before]
    for friend in friends:
        pl.semaphore_signal(barrier, inc=1, device_id=friend, device_id_type=MESH)
    pl.semaphore_wait(barrier, len(friends))

    def remote(src, dst, send_sem, recv_sem, device):
        return pltpu.make_async_remote_copy(src_ref=src, dst_ref=dst, send_sem=send_sem, recv_sem=recv_sem,
                                            device_id=device, device_id_type=MESH)

    def zx_copy(m):
        c = 2 * m + z
        return remote(tokens.at[m], x_in.at[c], zx_sem.at[m], in_sem.at[c], z_peer)

    def next_copy(c):
        return remote(x_out.at[c], x_in.at[c], next_send.at[c], in_sem.at[c], after)

    @pl.when(phase == 0)
    def _():
        for m in range(micro):
            zx_copy(m).start()
        for m in range(micro):
            x_in[2 * m + z] = tokens[m]

    sends = []

    def send(*args):
        copy = remote(*args)
        copy.start()
        sends.append(copy)

    first_axis, second_axis = ("x", "y"), ("y", "x")
    first, second = (x, y), (y, x)
    HOPS = (2, 1, 3)
    WAY = (1, 3)

    def slot(c, h, s, f):
        return gathered.at[c, s % SIDE, f % SIDE] if h == 0 else gathered.at[c, f % SIDE, s % SIDE]

    def enter(c):
        @pl.when((phase == 0) & (z != c % 2))
        def _():
            remote(tokens.at[c // 2], x_in.at[c], zx_sem.at[c // 2], in_sem.at[c], z_peer).wait_recv()

        @pl.when(phase > 0)
        def _():
            next_copy(c).wait_recv()

        wide = x_in[c].astype(F32)
        mean = jnp.mean(wide, axis=-1, keepdims=True)
        centered = wide - mean
        var = jnp.mean(centered * centered, axis=-1, keepdims=True)
        gathered[c, y, x] = (centered * lax.rsqrt(var + 1e-05) * gain[...]).astype(BF16)
        for t in HOPS:
            for h in range(2):
                block = slot(c, h, second[h], first[h]).at[:, pl.ds(h * half, half)]
                send(block, block, ag1_send.at[c, h, t - 1], ag1_recv.at[c, h, t - 1], along(first_axis[h], t))
        for h in range(2):
            relay(c, h, 0)

    def near_block(c, h, back):
        return slot(c, h, second[h], first[h] + SIDE - back).at[:, pl.ds(h * half, half)]

    def relay(c, h, back):
        block = near_block(c, h, back)
        for d in range(2):
            send(block, block, ag2_send.at[c, h, d, back], ag2_recv.at[c, h, d, back], along(second_axis[h], WAY[d]))

    def pass_on(c, back):
        for h in range(2):
            block = slot(c, h, 0, 0).at[:, pl.ds(0, half)]
            remote(block, block, ag1_send.at[c, h, back - 1], ag1_recv.at[c, h, back - 1], z_peer).wait_recv()
            relay(c, h, back)

    def forward(c, back):
        for d in range(2):
            for h in range(2):
                block = slot(c, h, 0, 0).at[:, pl.ds(0, half)]
                remote(block, block, ag2_send.at[c, h, d, back], ag2_recv.at[c, h, d, back], z_peer).wait_recv()
                block = slot(c, h, second[h] + SIDE - WAY[d], first[h] + SIDE - back).at[:, pl.ds(h * half + d * quarter, quarter)]
                send(block, block, ag3_send.at[c, h, d, back], ag3_recv.at[c, h, d, back], along(second_axis[h], WAY[d]))

    def collect(c):
        for back in range(SIDE):
            for d in range(2):
                for h in range(2):
                    block = slot(c, h, 0, 0).at[:, pl.ds(0, quarter)]
                    remote(block, block, ag3_send.at[c, h, d, back], ag3_recv.at[c, h, d, back], z_peer).wait_recv()

        def pack(i, carry):
            yy, xx = i // 2, (i % 2) * 2
            pair = jnp.concatenate([gathered[c, yy, xx].astype(F32), gathered[c, yy, xx + 1].astype(F32)], axis=0)
            lhs[pl.ds(pl.multiple_of(i * 2 * ROWS, 2 * ROWS), 2 * ROWS), :] = pair.astype(BF16)
            return carry

        lax.fori_loop(0, rows // (2 * ROWS), pack, 0)

    def up(c):
        if c == 0:
            up_copy.wait()
        wide_n = min(256, units)

        def tile(n, carry):
            columns = pl.ds(pl.multiple_of(n * wide_n, wide_n), wide_n)
            value = jnp.dot(lhs[...], w_up[:, columns], preferred_element_type=F32) + b_up[:, columns]
            hidden[:, columns] = jax.nn.gelu(value).astype(BF16)
            return carry

        lax.fori_loop(0, units // wide_n, tile, 0)

    def strip(c, h, part, s):
        return partial.at[c, h, part, s % SIDE]

    def reduce_send(c, h, stage, src, dst, d, index):
        send(src, dst, rs_send.at[c, h, stage, d, index], rs_recv.at[c, h, stage, d, index],
             along(second_axis[h], WAY[d]))

    def got(c, h, stage, d, index, ref):
        remote(ref, ref, rs_send.at[c, h, stage, d, index], rs_recv.at[c, h, stage, d, index], z_peer).wait_recv()

    def down(c, part):
        if c == 0 and part == 0:
            down_copy.wait()
        wide_q = min(512, quarter)
        for h in range(2):
            base = h * half + part * quarter

            def tile(n, carry):
                start = pl.multiple_of(n * wide_q, wide_q)
                value = jnp.dot(hidden[...], w_down[:, pl.ds(base + start, wide_q)], preferred_element_type=F32)
                value = value.reshape(SIDE, SIDE, ROWS, wide_q).astype(BF16)
                for i in range(SIDE):
                    if h == 0:
                        partial[c, h, part, i, :, :, pl.ds(start, wide_q)] = value[i]
                    else:
                        partial[c, h, part, :, i, :, pl.ds(start, wide_q)] = value[i]
                return carry

            lax.fori_loop(0, quarter // wide_q, tile, 0)
            reduce_send(c, h, 0, strip(c, h, part, second[h] + 2), far1.at[c, h, part], part, 0)
            reduce_send(c, h, 0, strip(c, h, part, second[h] + WAY[1 - part]), near1.at[c, h, 1 - part, part],
                        1 - part, 1 + part)

    def merge(c, part):
        for h in range(2):
            got(c, h, 0, part, 0, far1.at[c, h, part])
            target = strip(c, h, part, second[h] + WAY[part])

            def fold(i, carry):
                target[i] = (target[i].astype(F32) + far1[c, h, part, i].astype(F32)).astype(BF16)
                return carry

            lax.fori_loop(0, SIDE, fold, 0)
            reduce_send(c, h, 0, target, near1.at[c, h, part, part], part, 1 + part)

    def reduce1(c, part):
        for h in range(2):
            for d in range(2):
                got(c, h, 0, d, 1 + part, near1.at[c, h, d, part])
            mine = strip(c, h, part, second[h])

            def fold(i, carry):
                total = mine[i].astype(F32)
                for d in range(2):
                    total = total + near1[c, h, d, part, i].astype(F32)
                sum1[c, h, part, i] = total.astype(BF16)
                return carry

            lax.fori_loop(0, SIDE, fold, 0)
            for t in HOPS:
                send(sum1.at[c, h, part, (first[h] + t) % SIDE], near2.at[c, h, t - 1, part],
                     rs_send.at[c, h, 1, t - 1, part], rs_recv.at[c, h, 1, t - 1, part], along(first_axis[h], t))

    def z_copy(c, h, part):
        return remote(z_own.at[c, h, part], z_got.at[c, h, part], z_send.at[c, h, part], z_recv.at[c, h, part], z_peer)

    def reduce2(c, part):
        if True:
            for h in range(2):
                for t in HOPS:
                    ref = near2.at[c, h, t - 1, part]
                    remote(ref, ref, rs_send.at[c, h, 1, t - 1, part], rs_recv.at[c, h, 1, t - 1, part], z_peer).wait_recv()
                total = sum1[c, h, part, first[h]].astype(F32)
                for t in range(3):
                    total = total + near2[c, h, t, part].astype(F32)
                z_own[c, h, part] = total.astype(BF16)
                copy = z_copy(c, h, part)
                copy.start()
                sends.append(copy)

    def leave(c):
        for part in range(2):
            for h in range(2):
                z_copy(c, h, part).wait_recv()
                branch = z_own[c, h, part].astype(F32) + z_got[c, h, part].astype(F32)
                columns = pl.ds(h * half + part * quarter, quarter)
                x_out[c, :, columns] = (x_in[c, :, columns].astype(F32) + branch + b_down[:, columns]).astype(BF16)

        @pl.when(phase < phases - 1)
        def _():
            next_copy(c).start()

        @pl.when(z == c % 2)
        def _():
            out[0, c // 2] = x_out[c]

    steps = {"X": (enter,), "a": (pass_on, 1), "b": (pass_on, 3), "c": (pass_on, 2), "G": (collect,), "U": (up,), "D": (down, 0), "E": (down, 1),
             "e": (forward, 0), "f": (forward, 1), "g": (forward, 3), "h": (forward, 2), "m": (merge, 0), "n": (merge, 1),
             "p": (reduce1, 0), "r": (reduce1, 1), "q": (reduce2, 0), "s": (reduce2, 1), "Z": (leave,)}
    for step in ORDER:
        fn, *more = steps[step[0]]
        fn(int(step[1]), *more)

    for copy in sends:
        copy.wait_send()

    @pl.when(phase == 0)
    def _():
        for m in range(micro):
            zx_copy(m).wait_send()

    @pl.when(phase < phases - 1)
    def _():
        for c in range(chunks):
            next_copy(c).wait_send()


def on_device(phases, tokens, norm_gain, up_weight, up_bias, down_weight, down_bias):
    micro, own, depth = tokens.shape
    units = up_weight.shape[2]
    quarter = depth // 4
    chunks = 2 * micro
    vmem = pl.BlockSpec(memory_space=pltpu.VMEM)
    hbm = pl.BlockSpec(memory_space=pl.ANY)
    dma = pltpu.SemaphoreType.DMA
    return pl.pallas_call(
        functools.partial(kernel, phases),
        out_shape=jax.ShapeDtypeStruct((1, micro, own, depth), BF16),
        in_specs=[vmem, vmem, vmem, vmem, hbm, hbm],
        out_specs=vmem,
        scratch_shapes=[
            pltpu.VMEM((depth, units), BF16),
            pltpu.VMEM((units, depth), BF16),
            pltpu.VMEM((chunks, ROWS, depth), BF16),
            pltpu.VMEM((chunks, SIDE, SIDE, ROWS, depth), BF16),
            pltpu.VMEM((ROWS * SIDE * SIDE, depth), BF16),
            pltpu.VMEM((ROWS * SIDE * SIDE, units), BF16),
            pltpu.VMEM((chunks, 2, 2, SIDE, SIDE, ROWS, quarter), BF16),
            pltpu.VMEM((chunks, 2, 2, SIDE, ROWS, quarter), BF16),
            pltpu.VMEM((chunks, 2, 2, 2, SIDE, ROWS, quarter), BF16),
            pltpu.VMEM((chunks, 2, 2, SIDE, ROWS, quarter), BF16),
            pltpu.VMEM((chunks, 2, 3, 2, ROWS, quarter), BF16),
            pltpu.VMEM((chunks, 2, 2, ROWS, quarter), BF16),
            pltpu.VMEM((chunks, 2, 2, ROWS, quarter), BF16),
            pltpu.VMEM((chunks, ROWS, depth), BF16),
            dma((2,)),
            dma((micro,)),
            dma((chunks,)),
            dma((chunks, 2, 3)),
            dma((chunks, 2, 3)),
            dma((chunks, 2, 2, 4)),
            dma((chunks, 2, 2, 4)),
            dma((chunks, 2, 2, 4)),
            dma((chunks, 2, 2, 4)),
            dma((chunks, 2, 2, 3, 3)),
            dma((chunks, 2, 2, 3, 3)),
            dma((chunks, 2, 2)),
            dma((chunks, 2, 2)),
            dma((chunks,)),
        ],
        compiler_params=pltpu.CompilerParams(
            collective_id=0, has_side_effects=True, vmem_limit_bytes=60 * 1024 * 1024),
        name="relay",
    )(tokens, norm_gain, up_bias, down_bias, up_weight, down_weight)


def solution(mesh):
    return jax.shard_map(
        functools.partial(on_device, mesh.shape["phase"]),
        mesh=mesh,
        in_specs=(
            P(None, "blk", None),
            P("phase", None),
            P("phase", None, "blk"),
            P("phase", "blk"),
            P("phase", "blk", None),
            P("phase", None),
        ),
        out_specs=P("phase", None, "blk", None),
        check_vma=False,
    )
```

```python
import functools

import jax
import jax.numpy as jnp
from jax import lax
from jax.experimental import pallas as pl
from jax.experimental.pallas import tpu as pltpu
from jax.sharding import PartitionSpec as P

MESH = pl.DeviceIdType.MESH
SIDE = 4
ROWS = 8
F32, BF16 = jnp.float32, jnp.bfloat16
ORDER = (
    "X0", "X1", "a0", "b0", "c0", "e0", "a1", "X2", "f0", "g0", "h0", "b1", "c1", "e1", "a2", "b2",
    "c2", "X3", "G0", "f1", "U0", "g1", "h1", "e2", "D0", "a3", "b3", "c3", "f2", "g2", "h2", "E0",
    "G1", "U1", "e3", "D1", "f3", "m0", "g3", "h3", "E1", "G2", "U2", "n0", "m1", "D2", "E2", "G3",
    "n1", "U3", "p1", "p0", "r0", "D3", "m2", "r1", "n2", "E3", "q0", "s0", "q1", "m3", "p2", "s1",
    "r2", "Z0", "n3", "Z1", "q2", "p3", "s2", "r3", "Z2", "q3", "s3", "Z3",
)


def kernel(phases, tokens, gain, b_up, b_down, w_up_hbm, w_down_hbm, out,
           w_up, w_down, x_in, gathered, lhs, hidden, partial, far1, near1, sum1, near2, z_own, z_got, x_out,
           w_sem, zx_sem, in_sem, ag1_send, ag1_recv, ag2_send, ag2_recv, ag3_send, ag3_recv, rs_send, rs_recv, z_send, z_recv, next_send, next_recv):
    micro, _, depth = tokens.shape
    chunks = 2 * micro
    quarter = depth // 4
    half = depth // 2
    units = w_up.shape[1]
    rows = ROWS * SIDE * SIDE
    phase = lax.axis_index("phase")
    blk = lax.axis_index("blk")
    y, z, x = blk // 8, (blk // 4) % 2, blk % 4

    def at(yy, zz, xx):
        return (phase, ((yy % SIDE) * 2 + zz) * 4 + xx % SIDE)

    def turned(odd):
        return jnp.where(odd == 1, y * 8 + (1 - z) * 4 + x, blk)

    def along(axis, t):
        return at(y, z, x + t) if axis == "x" else at(y + t, z, x)

    z_peer = at(y, 1 - z, x)
    after = ((phase + 1) % phases, turned(phase % 2))
    before = ((phase + phases - 1) % phases, turned((phase + 1) % 2))

    up_copy = pltpu.make_async_copy(w_up_hbm.at[0], w_up, w_sem.at[0])
    down_copy = pltpu.make_async_copy(w_down_hbm.at[0], w_down, w_sem.at[1])
    up_copy.start()
    down_copy.start()

    barrier = pltpu.get_barrier_semaphore()
    friends = [along(axis, t) for axis in "xy" for t in (1, 2, 3)] + [z_peer, after, before]
    for friend in friends:
        pl.semaphore_signal(barrier, inc=1, device_id=friend, device_id_type=MESH)
    pl.semaphore_wait(barrier, len(friends))

    def remote(src, dst, send_sem, recv_sem, device):
        return pltpu.make_async_remote_copy(src_ref=src, dst_ref=dst, send_sem=send_sem, recv_sem=recv_sem,
                                            device_id=device, device_id_type=MESH)

    def zx_copy(m):
        c = 2 * m + z
        return remote(tokens.at[m], x_in.at[c], zx_sem.at[m], in_sem.at[c], z_peer)

    def next_copy(c, q):
        cut = pl.ds(q * quarter, quarter)
        return remote(x_out.at[c, :, cut], x_in.at[c, :, cut], next_send.at[c, q], next_recv.at[c, q], after)

    @pl.when(phase == 0)
    def _():
        for m in range(micro):
            zx_copy(m).start()
        for m in range(micro):
            x_in[2 * m + z] = tokens[m]

    sends = []

    def send(*args):
        copy = remote(*args)
        copy.start()
        sends.append(copy)

    first_axis, second_axis = ("x", "y"), ("y", "x")
    first, second = (x, y), (y, x)
    HOPS = (2, 1, 3)
    WAY = (1, 3)

    def slot(c, h, s, f):
        return gathered.at[c, s % SIDE, f % SIDE] if h == 0 else gathered.at[c, f % SIDE, s % SIDE]

    def enter(c):
        @pl.when((phase == 0) & (z != c % 2))
        def _():
            remote(tokens.at[c // 2], x_in.at[c], zx_sem.at[c // 2], in_sem.at[c], z_peer).wait_recv()

        @pl.when(phase > 0)
        def _():
            for q in range(4):
                next_copy(c, q).wait_recv()

        wide = x_in[c].astype(F32)
        mean = jnp.mean(wide, axis=-1, keepdims=True)
        centered = wide - mean
        var = jnp.mean(centered * centered, axis=-1, keepdims=True)
        gathered[c, y, x] = (centered * lax.rsqrt(var + 1e-05) * gain[...]).astype(BF16)
        for t in HOPS:
            for h in range(2):
                block = slot(c, h, second[h], first[h]).at[:, pl.ds(h * half, half)]
                send(block, block, ag1_send.at[c, h, t - 1], ag1_recv.at[c, h, t - 1], along(first_axis[h], t))
        for h in range(2):
            relay(c, h, 0)

    def near_block(c, h, back):
        return slot(c, h, second[h], first[h] + SIDE - back).at[:, pl.ds(h * half, half)]

    def relay(c, h, back):
        block = near_block(c, h, back)
        for d in range(2):
            send(block, block, ag2_send.at[c, h, d, back], ag2_recv.at[c, h, d, back], along(second_axis[h], WAY[d]))

    def pass_on(c, back):
        for h in range(2):
            block = slot(c, h, 0, 0).at[:, pl.ds(0, half)]
            remote(block, block, ag1_send.at[c, h, back - 1], ag1_recv.at[c, h, back - 1], z_peer).wait_recv()
            relay(c, h, back)

    def forward(c, back):
        for d in range(2):
            for h in range(2):
                block = slot(c, h, 0, 0).at[:, pl.ds(0, half)]
                remote(block, block, ag2_send.at[c, h, d, back], ag2_recv.at[c, h, d, back], z_peer).wait_recv()
                block = slot(c, h, second[h] + SIDE - WAY[d], first[h] + SIDE - back).at[:, pl.ds(h * half + d * quarter, quarter)]
                send(block, block, ag3_send.at[c, h, d, back], ag3_recv.at[c, h, d, back], along(second_axis[h], WAY[d]))

    def collect(c):
        for back in range(SIDE):
            for d in range(2):
                for h in range(2):
                    block = slot(c, h, 0, 0).at[:, pl.ds(0, quarter)]
                    remote(block, block, ag3_send.at[c, h, d, back], ag3_recv.at[c, h, d, back], z_peer).wait_recv()

        def pack(i, carry):
            yy, xx = i // 2, (i % 2) * 2
            pair = jnp.concatenate([gathered[c, yy, xx].astype(F32), gathered[c, yy, xx + 1].astype(F32)], axis=0)
            lhs[pl.ds(pl.multiple_of(i * 2 * ROWS, 2 * ROWS), 2 * ROWS), :] = pair.astype(BF16)
            return carry

        lax.fori_loop(0, rows // (2 * ROWS), pack, 0)

    def up(c):
        if c == 0:
            up_copy.wait()
        wide_n = min(256, units)

        def tile(n, carry):
            columns = pl.ds(pl.multiple_of(n * wide_n, wide_n), wide_n)
            value = jnp.dot(lhs[...], w_up[:, columns], preferred_element_type=F32) + b_up[:, columns]
            hidden[:, columns] = jax.nn.gelu(value).astype(BF16)
            return carry

        lax.fori_loop(0, units // wide_n, tile, 0)

    def strip(c, h, part, s):
        return partial.at[c, h, part, s % SIDE]

    def reduce_send(c, h, stage, src, dst, d, index):
        send(src, dst, rs_send.at[c, h, stage, d, index], rs_recv.at[c, h, stage, d, index],
             along(second_axis[h], WAY[d]))

    def got(c, h, stage, d, index, ref):
        remote(ref, ref, rs_send.at[c, h, stage, d, index], rs_recv.at[c, h, stage, d, index], z_peer).wait_recv()

    def down(c, part):
        if c == 0 and part == 0:
            down_copy.wait()
        wide_q = min(512, quarter)
        for h in range(2):
            base = h * half + part * quarter

            def tile(n, carry):
                start = pl.multiple_of(n * wide_q, wide_q)
                value = jnp.dot(hidden[...], w_down[:, pl.ds(base + start, wide_q)], preferred_element_type=F32)
                value = value.reshape(SIDE, SIDE, ROWS, wide_q).astype(BF16)
                for i in range(SIDE):
                    if h == 0:
                        partial[c, h, part, i, :, :, pl.ds(start, wide_q)] = value[i]
                    else:
                        partial[c, h, part, :, i, :, pl.ds(start, wide_q)] = value[i]
                return carry

            lax.fori_loop(0, quarter // wide_q, tile, 0)
            reduce_send(c, h, 0, strip(c, h, part, second[h] + 2), far1.at[c, h, part], part, 0)
            reduce_send(c, h, 0, strip(c, h, part, second[h] + WAY[1 - part]), near1.at[c, h, 1 - part, part],
                        1 - part, 1 + part)

    def merge(c, part):
        for h in range(2):
            got(c, h, 0, part, 0, far1.at[c, h, part])
            target = strip(c, h, part, second[h] + WAY[part])

            def fold(i, carry):
                target[i] = (target[i].astype(F32) + far1[c, h, part, i].astype(F32)).astype(BF16)
                return carry

            lax.fori_loop(0, SIDE, fold, 0)
            reduce_send(c, h, 0, target, near1.at[c, h, part, part], part, 1 + part)

    def reduce1(c, part):
        for h in range(2):
            for d in range(2):
                got(c, h, 0, d, 1 + part, near1.at[c, h, d, part])
            mine = strip(c, h, part, second[h])

            def fold(i, carry):
                total = mine[i].astype(F32)
                for d in range(2):
                    total = total + near1[c, h, d, part, i].astype(F32)
                sum1[c, h, part, i] = total.astype(BF16)
                return carry

            lax.fori_loop(0, SIDE, fold, 0)
            for t in HOPS:
                send(sum1.at[c, h, part, (first[h] + t) % SIDE], near2.at[c, h, t - 1, part],
                     rs_send.at[c, h, 1, t - 1, part], rs_recv.at[c, h, 1, t - 1, part], along(first_axis[h], t))

    def z_copy(c, h, part):
        return remote(z_own.at[c, h, part], z_got.at[c, h, part], z_send.at[c, h, part], z_recv.at[c, h, part], z_peer)

    def reduce2(c, part):
        if True:
            for h in range(2):
                for t in HOPS:
                    ref = near2.at[c, h, t - 1, part]
                    remote(ref, ref, rs_send.at[c, h, 1, t - 1, part], rs_recv.at[c, h, 1, t - 1, part], z_peer).wait_recv()
                total = sum1[c, h, part, first[h]].astype(F32)
                for t in range(3):
                    total = total + near2[c, h, t, part].astype(F32)
                z_own[c, h, part] = total.astype(BF16)
                copy = z_copy(c, h, part)
                copy.start()
                sends.append(copy)

    def leave(c):
        for part in range(2):
            for h in range(2):
                z_copy(c, h, part).wait_recv()
                branch = z_own[c, h, part].astype(F32) + z_got[c, h, part].astype(F32)
                columns = pl.ds(h * half + part * quarter, quarter)
                x_out[c, :, columns] = (x_in[c, :, columns].astype(F32) + branch + b_down[:, columns]).astype(BF16)

                @pl.when(phase < phases - 1)
                def _():
                    next_copy(c, 2 * h + part).start()

        @pl.when(z == c % 2)
        def _():
            out[0, c // 2] = x_out[c]

    steps = {"X": (enter,), "a": (pass_on, 1), "b": (pass_on, 3), "c": (pass_on, 2), "G": (collect,), "U": (up,), "D": (down, 0), "E": (down, 1),
             "e": (forward, 0), "f": (forward, 1), "g": (forward, 3), "h": (forward, 2), "m": (merge, 0), "n": (merge, 1),
             "p": (reduce1, 0), "r": (reduce1, 1), "q": (reduce2, 0), "s": (reduce2, 1), "Z": (leave,)}
    for step in ORDER:
        fn, *more = steps[step[0]]
        fn(int(step[1]), *more)

    for copy in sends:
        copy.wait_send()

    @pl.when(phase == 0)
    def _():
        for m in range(micro):
            zx_copy(m).wait_send()

    @pl.when(phase < phases - 1)
    def _():
        for c in range(chunks):
            for q in range(4):
                next_copy(c, q).wait_send()


def on_device(phases, tokens, norm_gain, up_weight, up_bias, down_weight, down_bias):
    micro, own, depth = tokens.shape
    units = up_weight.shape[2]
    quarter = depth // 4
    chunks = 2 * micro
    vmem = pl.BlockSpec(memory_space=pltpu.VMEM)
    hbm = pl.BlockSpec(memory_space=pl.ANY)
    dma = pltpu.SemaphoreType.DMA
    return pl.pallas_call(
        functools.partial(kernel, phases),
        out_shape=jax.ShapeDtypeStruct((1, micro, own, depth), BF16),
        in_specs=[vmem, vmem, vmem, vmem, hbm, hbm],
        out_specs=vmem,
        scratch_shapes=[
            pltpu.VMEM((depth, units), BF16),
            pltpu.VMEM((units, depth), BF16),
            pltpu.VMEM((chunks, ROWS, depth), BF16),
            pltpu.VMEM((chunks, SIDE, SIDE, ROWS, depth), BF16),
            pltpu.VMEM((ROWS * SIDE * SIDE, depth), BF16),
            pltpu.VMEM((ROWS * SIDE * SIDE, units), BF16),
            pltpu.VMEM((chunks, 2, 2, SIDE, SIDE, ROWS, quarter), BF16),
            pltpu.VMEM((chunks, 2, 2, SIDE, ROWS, quarter), BF16),
            pltpu.VMEM((chunks, 2, 2, 2, SIDE, ROWS, quarter), BF16),
            pltpu.VMEM((chunks, 2, 2, SIDE, ROWS, quarter), BF16),
            pltpu.VMEM((chunks, 2, 3, 2, ROWS, quarter), BF16),
            pltpu.VMEM((chunks, 2, 2, ROWS, quarter), BF16),
            pltpu.VMEM((chunks, 2, 2, ROWS, quarter), BF16),
            pltpu.VMEM((chunks, ROWS, depth), BF16),
            dma((2,)),
            dma((micro,)),
            dma((chunks,)),
            dma((chunks, 2, 3)),
            dma((chunks, 2, 3)),
            dma((chunks, 2, 2, 4)),
            dma((chunks, 2, 2, 4)),
            dma((chunks, 2, 2, 4)),
            dma((chunks, 2, 2, 4)),
            dma((chunks, 2, 2, 3, 3)),
            dma((chunks, 2, 2, 3, 3)),
            dma((chunks, 2, 2)),
            dma((chunks, 2, 2)),
            dma((chunks, 4)),
            dma((chunks, 4)),
        ],
        compiler_params=pltpu.CompilerParams(
            collective_id=0, has_side_effects=True, vmem_limit_bytes=60 * 1024 * 1024),
        name="relay",
    )(tokens, norm_gain, up_bias, down_bias, up_weight, down_weight)


def solution(mesh):
    return jax.shard_map(
        functools.partial(on_device, mesh.shape["phase"]),
        mesh=mesh,
        in_specs=(
            P(None, "blk", None),
            P("phase", None),
            P("phase", None, "blk"),
            P("phase", "blk"),
            P("phase", "blk", None),
            P("phase", None),
        ),
        out_specs=P("phase", None, "blk", None),
        check_vma=False,
    )
```
